32 devices in a mesh: seq: 2 (over x), fsdp: 16 (over z, y, core).
Axes of the slice: x: 2, y: 2, z: 4, core: 2. Of those that a mesh axis runs over, the one named last changes fastest.
Arguments:
- incoming_state: bfloat16 [16, 512, 768], P('fsdp', 'seq'), may hold values from -6 to 6
- projection_matrix_triple: bfloat16 [768, 2304], P(('seq', 'fsdp')), may hold values from -0.3125 to 0.3125
- merge_matrix: bfloat16 [768, 768], P(('seq', 'fsdp')), may hold values from -1.75 to 1.75
- widen_matrix: bfloat16 [768, 3072], P(('seq', 'fsdp')), may hold values from -0.21875 to 0.21875
- shrink_matrix: bfloat16 [3072, 768], P(('seq', 'fsdp')), may hold values from -0.109375 to 0.109375
- offset_table: bfloat16 [6, 768], P(None, ('seq', 'fsdp')), may hold values from -1.5 to 1.5
- norm_scales: bfloat16 [2, 768], P(None, ('seq', 'fsdp')), may hold values from 0.25 to 1.75
- widen_offset: bfloat16 [3072], P(('seq', 'fsdp')), may hold values from -1.5 to 1.5
- trainable_gate_scores: float32 [12, 512, 512], P('seq', 'fsdp'), may hold values from -8 to 8
- gate_perturbation: float32 [12, 512, 512], P('seq', 'fsdp'), may hold values from -6 to 6
- softening_scale: float32 [12], P('seq'), may hold values from 0.5 to 2
- passage_extents: int32 [32], replicated, may hold values from 1 to 512, 8192 in all
- result_cotangent: bfloat16 [16, 512, 768], P('fsdp', 'seq'), may hold values from -6 to 6
Outputs:
- layer_out: bfloat16 [16, 512, 768], P('fsdp', 'seq')
- input_grad: float32 [16, 512, 768], P('fsdp', 'seq')
- grad_w_qkv: float32 [768, 2304], P(('seq', 'fsdp'))
- grad_w_out: float32 [768, 768], P(('seq', 'fsdp'))
- grad_w_up: float32 [768, 3072], P(('seq', 'fsdp'))
- grad_w_down: float32 [3072, 768], P(('seq', 'fsdp'))
- grad_biases: float32 [6, 768], P(None, ('seq', 'fsdp'))
- grad_gains: float32 [2, 768], P(None, ('seq', 'fsdp'))
- grad_bias_up: float32 [3072], P(('seq', 'fsdp'))
- mask_logit_gradient: float32 [12, 512, 512], P('seq', 'fsdp')
The draws below stay inside these ranges and needn't reach their ends.
Inputs may be any that keep to these rules, and one draw needn't show every extreme that they name: `passage_extents`: they sum to 8192, and the longest is exactly 512.
All inputs are finite; a program needn't handle non-finite values.
Results may differ from the reference program's by a relative error of at most 0.013.
Values may be sent and summed in bfloat16 or wider, within the bound.
No kernel may reach another device: no remote copies, remote signals or barrier semaphores. Data moves between devices by JAX's collectives and lax.ppermute only.
A program may use at most 192 MiB of HBM per device.

```python
import math
import jax
import jax.numpy as jnp
import numpy as np
from jax import lax

D = 768
FF = 3072
FOCUS_COUNT = 12
HDIM = 64
MPOS = 512
GROUP_TOK = 512
GROUPS = 16
TOKENS = 8192
DOC_MAX = 512
NDOCS = 32


def levels(stream_key, dims, shards, low, high):
    def one(dim, blocks):
        heights = jax.random.uniform(jax.random.fold_in(jax.random.fold_in(stream_key, 6), dim), (blocks,), jnp.float32, low / len(shards), high / len(shards))
        return jnp.repeat(jnp.exp(heights), dims[dim] // blocks).reshape((-1,) + (1,) * (len(dims) - dim - 1))

    level = one(*shards[0])
    for cut in shards[1:]:
        level = level * one(*cut)
    return level


def profile(count, total, reach, skew):
    loads = [(1 << 20) // math.isqrt(standing ** skew) + 1 for standing in range(2, count + 1)]
    spare, holding = total - reach - (count - 1), [1] * (count - 1)
    while spare > 0:
        candidates = [i for i in range(count - 1) if holding[i] < reach]
        pool, remaining = sum([loads[i] for i in candidates]), spare
        for i in candidates:
            extra = min(reach - holding[i], max(1, remaining * loads[i] // pool), spare)
            holding[i] = holding[i] + extra
            spare = spare - extra
    return np.array([reach] + holding)


def uneven(rng, number_of, total, limit, slope):
    if number_of == 2:
        one = jax.random.randint(rng, (), max(1, total - limit), min(limit, total - 1) + 1)
        return jnp.stack([one, total - one])
    tallies = jnp.asarray(profile(number_of, total, limit, slope), jnp.int32)
    couples = (number_of - 1) // 2
    source_of, sink = tallies[1:1 + 2 * couples:2], tallies[2:2 + 2 * couples:2]
    margin = jnp.minimum(source_of - 1, limit - sink)
    moved = jax.random.randint(jax.random.fold_in(rng, 1), (couples,), 0, 1 << 20) % (margin + 1)
    tallies = tallies.at[1:1 + 2 * couples:2].set(source_of - moved).at[2:2 + 2 * couples:2].set(sink + moved)
    return tallies[jax.random.permutation(jax.random.fold_in(rng, 2), number_of)]


def noise(own_key, extent, deviation, limit, split=(), kind=jnp.bfloat16):
    array = jax.random.normal(own_key, extent, jnp.float32) * deviation
    if len(split) > 0:
        array = levels(own_key, extent, split, -0.22, 0.18) * array
    return jnp.clip(array, min=-limit, max=limit).astype(kind)


def setup_inputs(seed: int = 0) -> dict:
    splits = jax.random.split(jax.random.key(seed), 14)
    return {
        "incoming_state": noise(splits[0], (GROUPS, GROUP_TOK, D), 1.0, 6.0, ((0, 16), (1, 2))),
        "projection_matrix_triple": noise(splits[1], (D, 3 * D), (D // 2) ** -0.5, 0.3125, ((0, 32),)),
        "merge_matrix": noise(splits[2], (D, D), (D // 64) ** -0.5, 1.75, ((0, 32),)),
        "widen_matrix": noise(splits[3], (D, FF), D ** -0.5, 0.21875, ((0, 32),)),
        "shrink_matrix": noise(splits[4], (FF, D), FF ** -0.5, 0.109375, ((0, 32),)),
        "offset_table": noise(splits[5], (6, D), 0.3, 1.5, ((1, 32),)),
        "norm_scales": jnp.clip(1.0 + 0.15 * jax.random.normal(splits[6], (2, D), jnp.float32), 0.25, 1.75).astype(jnp.bfloat16),
        "widen_offset": noise(splits[7], (FF,), 0.3, 1.5, ((0, 32),)),
        "trainable_gate_scores": noise(splits[8], (FOCUS_COUNT, MPOS, MPOS), 1.5, 8.0, ((0, 2), (1, 16)), jnp.float32),
        "gate_perturbation": noise(splits[9], (FOCUS_COUNT, MPOS, MPOS), 1.0, 6.0, ((0, 2), (1, 16)), jnp.float32),
        "softening_scale": jnp.clip(jnp.exp(math.log(2.0) - 1.3862944 * jax.random.uniform(splits[10], (FOCUS_COUNT,), jnp.float32) ** levels(splits[10], (FOCUS_COUNT,), ((0, 2),), -0.2, 0.2)), 0.5, 2.0),
        "passage_extents": uneven(splits[11], NDOCS, TOKENS, DOC_MAX, 2).astype(jnp.int32),
        "result_cotangent": noise(splits[12], (GROUPS, GROUP_TOK, D), 1.0, 6.0, ((0, 16), (1, 2))),
    }


EPS = 1e-05
HIGH = lax.Precision.HIGHEST

@jax.custom_vjp
def low(v):
    return lax.optimization_barrier(v.astype(jnp.bfloat16)).astype(jnp.float32)

@jax.custom_vjp
def low_back(v):
    return v

def low_keep(v):
    return (low(v), None)

def low_pass(kept, grad):
    return (grad,)

def back_keep(v):
    return (v, None)

def back_low(kept, grad):
    return (low(grad),)
low.defvjp(low_keep, low_pass)
low_back.defvjp(back_keep, back_low)

def matmul_high(left, right):
    return jnp.dot(left, right, precision=HIGH, preferred_element_type=jnp.float32)

def layer_norm(values, gain, shift):
    center = values - lax.optimization_barrier(jnp.mean(values, axis=-1, keepdims=True))
    spread = lax.optimization_barrier(jnp.mean(center * center, axis=-1, keepdims=True))
    return center * lax.rsqrt(spread + EPS) * gain + shift

def locate(index, passage_opening, passage_finish, stream_rows):
    document = lax.optimization_barrier(jnp.sum((passage_finish[None, :] <= index[:, None]).astype(jnp.int32), axis=1)).astype(jnp.int32)
    begin = lax.optimization_barrier(jnp.max(jnp.where(passage_opening[None, :] <= index[:, None], passage_opening[None, :], 0), axis=1)).astype(jnp.int32)
    inside = (index >= 0) & (index < stream_rows)
    document = jnp.where(inside, document, -1).astype(jnp.int32)
    position = ((index - begin) % MPOS).astype(jnp.int32)
    return (document, position)

def block_evaluate(block_arguments, projection_matrix_triple, merge_matrix, widen_matrix, shrink_matrix, offset_table, norm_scales, widen_offset, trainable_gate_scores, gate_perturbation, softening_scale, passage_opening, passage_finish):
    stream_rows = block_arguments.shape[0]
    group_rows = GROUP_TOK
    smooth_gate = low(jax.nn.sigmoid((trainable_gate_scores + gate_perturbation) / softening_scale[:, None, None]))
    qkv_bias = jnp.concatenate([offset_table[0], jnp.zeros_like(offset_table[0]), offset_table[1]])
    qkv = low_back(low(matmul_high(block_arguments, projection_matrix_triple) + qkv_bias))
    query = qkv[:, :D].reshape(stream_rows, FOCUS_COUNT, HDIM)
    key = qkv[:, D:2 * D].reshape(stream_rows, FOCUS_COUNT, HDIM)
    value = qkv[:, 2 * D:].reshape(stream_rows, FOCUS_COUNT, HDIM)
    padding = jnp.zeros((group_rows, FOCUS_COUNT, HDIM), qkv.dtype)
    key_pad = jnp.concatenate([padding, key, padding], axis=0)
    value_pad = jnp.concatenate([padding, value, padding], axis=0)

    def attend(block):
        first = block * group_rows
        query_block = lax.dynamic_slice_in_dim(query, first, group_rows, 0)
        key_block = lax.dynamic_slice_in_dim(key_pad, first, 3 * group_rows, 0)
        value_block = lax.dynamic_slice_in_dim(value_pad, first, 3 * group_rows, 0)
        query_doc, query_pos = locate(first + jnp.arange(group_rows, dtype=jnp.int32), passage_opening, passage_finish, stream_rows)
        key_doc, key_pos = locate(first - group_rows + jnp.arange(3 * group_rows, dtype=jnp.int32), passage_opening, passage_finish, stream_rows)
        scores = low_back(jnp.einsum('qhd,khd->hqk', query_block, key_block, precision=HIGH) * 0.125)
        scores = jnp.where((query_doc[:, None] == key_doc[None, :])[None], scores, -1e+30)
        row_top = lax.optimization_barrier(jnp.max(scores, axis=-1, keepdims=True))
        weights = jnp.exp(scores - row_top)
        probs = weights / lax.optimization_barrier(jnp.sum(weights, axis=-1, keepdims=True))
        lookup = jnp.take(jnp.take(smooth_gate, query_pos, axis=1), key_pos, axis=2)
        mixed = low(probs * lookup)
        return jnp.einsum('hqk,khd->qhd', mixed, value_block, precision=HIGH)
    blocks = stream_rows // group_rows
    context = lax.map(jax.checkpoint(attend), jnp.arange(blocks, dtype=jnp.int32))
    context = low_back(low(context.reshape(stream_rows, D)))
    attn = low_back(matmul_high(context, merge_matrix) + offset_table[2])
    normed = layer_norm(block_arguments + attn, norm_scales[0], offset_table[4])
    up = low_back(matmul_high(low(normed), widen_matrix) + widen_offset)
    act = low(jax.nn.gelu(up, approximate=False))
    down = low_back(matmul_high(act, shrink_matrix) + offset_table[3])
    return layer_norm(normed + down, norm_scales[1], offset_table[5])

def reference(incoming_state, projection_matrix_triple, merge_matrix, widen_matrix, shrink_matrix, offset_table, norm_scales, widen_offset, trainable_gate_scores, gate_perturbation, softening_scale, passage_extents, result_cotangent):
    passage_finish = jnp.cumsum(passage_extents).astype(jnp.int32)
    passage_opening = (passage_finish - passage_extents).astype(jnp.int32)
    block_arguments = incoming_state.reshape(-1, D).astype(jnp.float32)

    def layer(block_arguments, projection_matrix_triple, merge_matrix, widen_matrix, shrink_matrix, offset_table, norm_scales, widen_offset, trainable_gate_scores):
        return block_evaluate(block_arguments, projection_matrix_triple, merge_matrix, widen_matrix, shrink_matrix, offset_table, norm_scales, widen_offset, trainable_gate_scores, gate_perturbation, softening_scale, passage_opening, passage_finish)
    output, pullback = jax.vjp(layer, block_arguments, projection_matrix_triple.astype(jnp.float32), merge_matrix.astype(jnp.float32), widen_matrix.astype(jnp.float32), shrink_matrix.astype(jnp.float32), offset_table.astype(jnp.float32), norm_scales.astype(jnp.float32), widen_offset.astype(jnp.float32), trainable_gate_scores)
    grads = pullback(result_cotangent.reshape(-1, D).astype(jnp.float32))
    return (output.astype(jnp.bfloat16).reshape(incoming_state.shape), grads[0].reshape(incoming_state.shape), grads[1], grads[2], grads[3], grads[4], grads[5], grads[6], grads[7], grads[8])
```

```python
from functools import partial

import jax
import jax.numpy as jnp
from jax import lax
from jax.experimental import pallas as pl
from jax.experimental.pallas import tpu as pltpu
from jax.sharding import PartitionSpec as P

D = 768
FOCUS_COUNT = 12
HDIM = 64
MPOS = 512
EPS = 1e-05
BLOCK = 512
PAIR = 128
TILE = 128
PIECE = 32
BOTH = ("seq", "fsdp")
BF = jnp.bfloat16
F32 = jnp.float32


def layer_norm(values, gain, shift):
    center = values - jnp.mean(values, axis=-1, keepdims=True)
    spread = jnp.mean(center * center, axis=-1, keepdims=True)
    return center * lax.rsqrt(spread + EPS) * gain + shift


def plain_dot(left, right):
    return jnp.dot(left, right, preferred_element_type=F32)


def left_dot(left, right):
    return lax.dot_general(left, right, (((0,), (0,)), ((), ())), preferred_element_type=F32)


def right_dot(left, right):
    return lax.dot_general(left, right, (((1,), (1,)), ((), ())), preferred_element_type=F32)


def two_heads(rows):
    lane = lax.broadcasted_iota(jnp.int32, rows.shape, 1)
    zero = jnp.zeros_like(rows)
    return jnp.concatenate(
        [jnp.where(lane < HDIM, rows, zero), jnp.where(lane < HDIM, zero, rows)], axis=0
    ).astype(BF)


def one_row_set(pairs):
    half = pairs.shape[0] // 2
    lane = lax.broadcasted_iota(jnp.int32, (half, pairs.shape[1]), 1)
    return jnp.where(lane < HDIM, pairs[:half], pairs[half:])


def for_documents(extent_ref, info_ref, visit):
    first = info_ref[0]

    def step(index, begin):
        length = extent_ref[index]
        finish = begin + length

        @pl.when((begin < first + BLOCK) & (finish > first))
        def _():
            visit(begin - first + BLOCK, length)

        return finish

    lax.fori_loop(0, extent_ref.shape[0], step, jnp.int32(0))


def table_rows(table_ref, info_ref, tile):
    parts = []
    for head in range(2):
        for piece in range(TILE // PIECE):
            where = info_ref[1 + tile * (TILE // PIECE) + piece]
            parts.append(table_ref[where, head])
    return jnp.concatenate(parts, axis=0).astype(F32)


def weights_of(queries, keys, length):
    scores = right_dot(queries, keys)
    column = lax.broadcasted_iota(jnp.int32, scores.shape, 1)
    scores = jnp.where(column < length, scores, -1e30)
    weights = jnp.exp(scores - jnp.max(scores, axis=1, keepdims=True))
    return weights, jnp.sum(weights, axis=1, keepdims=True)


def fill_window(window, low, own, high):
    window[0:BLOCK, :] = low[...].astype(F32)
    window[BLOCK : 2 * BLOCK, :] = own[...].astype(F32)
    window[2 * BLOCK : 3 * BLOCK, :] = high[...].astype(F32)


def fill_middle(window, own, scale=None):
    value = own[...].astype(F32)
    zero = jnp.zeros((BLOCK, PAIR), F32)
    window[0:BLOCK, :] = zero
    window[BLOCK : 2 * BLOCK, :] = value if scale is None else value * scale
    window[2 * BLOCK : 3 * BLOCK, :] = zero


def forward_kernel(
    extent_ref, info_ref, q_ref, k_ref, v_ref, lk_ref, lv_ref, hk_ref, hv_ref, table_ref, out_ref,
    q_win, k_win, v_win, o_win, k_doc, v_doc,
):
    fill_middle(q_win, q_ref, 0.125)
    fill_window(k_win, lk_ref, k_ref, hk_ref)
    fill_window(v_win, lv_ref, v_ref, hv_ref)

    def visit(offset, length):
        k_doc[...] = k_win[pl.ds(offset, MPOS), :].astype(BF)
        v_doc[...] = v_win[pl.ds(offset, MPOS), :].astype(BF)
        start = jnp.maximum(0, BLOCK - offset)
        finish = jnp.minimum(length, 2 * BLOCK - offset)

        def tile(index, carry):
            at = pl.ds(offset + index * TILE, TILE)
            weights, total = weights_of(two_heads(q_win[at, :]), k_doc[...], length)
            mixed = (weights * table_rows(table_ref, info_ref, index)).astype(BF)
            o_win[at, :] = one_row_set(plain_dot(mixed, v_doc[...]) / total)
            return carry

        lax.fori_loop(start // TILE, (finish + TILE - 1) // TILE, tile, 0)

    for_documents(extent_ref, info_ref, visit)
    out_ref[...] = o_win[BLOCK : 2 * BLOCK, :].astype(BF)


def backward_kernel(
    extent_ref, info_ref, q_ref, k_ref, v_ref, lk_ref, lv_ref, hk_ref, hv_ref, table_ref, g_ref,
    dq_ref, dk_ref, dv_ref, dt_ref,
    q_win, k_win, v_win, g_win, dq_win, dk_win, dv_win, dt_all, k_doc, v_doc, dk_doc, dv_doc,
):
    fill_middle(q_win, q_ref, 0.125)
    fill_middle(g_win, g_ref)
    fill_window(k_win, lk_ref, k_ref, hk_ref)
    fill_window(v_win, lv_ref, v_ref, hv_ref)
    dk_win[...] = jnp.zeros_like(dk_win)
    dv_win[...] = jnp.zeros_like(dv_win)
    dt_all[...] = jnp.zeros_like(dt_all)

    def visit(offset, length):
        k_doc[...] = k_win[pl.ds(offset, MPOS), :].astype(BF)
        v_doc[...] = v_win[pl.ds(offset, MPOS), :].astype(BF)
        dk_doc[...] = jnp.zeros_like(dk_doc)
        dv_doc[...] = jnp.zeros_like(dv_doc)
        start = jnp.maximum(0, BLOCK - offset)
        finish = jnp.minimum(length, 2 * BLOCK - offset)

        def tile(index, carry):
            at = pl.ds(offset + index * TILE, TILE)
            queries = two_heads(q_win[at, :])
            grads = two_heads(g_win[at, :])
            weights, total = weights_of(queries, k_doc[...], length)
            place = lax.broadcasted_iota(jnp.int32, (2, TILE, 1), 1).reshape(2 * TILE, 1)
            place = place + index * TILE
            probs = weights * jnp.where((place >= start) & (place < finish), 1.0 / total, 0.0)
            lookup = table_rows(table_ref, info_ref, index)
            mixed_grad = right_dot(grads, v_doc[...])
            mixed = probs * lookup
            lookup_grad = mixed_grad * probs
            delta = jnp.sum(lookup_grad * lookup, axis=1, keepdims=True)
            score_low = (probs * (mixed_grad * lookup - delta)).astype(BF)
            rows = pl.ds(pl.multiple_of(index * TILE, TILE), TILE)
            dt_all[0, rows, :] += lookup_grad[:TILE]
            dt_all[1, rows, :] += lookup_grad[TILE:]
            dq_win[at, :] = one_row_set(plain_dot(score_low, k_doc[...]) * 0.125)
            dk_doc[...] += left_dot(score_low, queries)
            dv_doc[...] += left_dot(mixed.astype(BF), grads)
            return carry

        lax.fori_loop(start // TILE, (finish + TILE - 1) // TILE, tile, 0)
        dk_win[pl.ds(offset, MPOS), :] = dk_doc[...]
        dv_win[pl.ds(offset, MPOS), :] = dv_doc[...]

    for_documents(extent_ref, info_ref, visit)
    dq_ref[...] = dq_win[BLOCK : 2 * BLOCK, :].astype(BF)
    dk_ref[...] = dk_win[...].astype(BF)
    dv_ref[...] = dv_win[...].astype(BF)
    dt_ref[...] = dt_all[...].astype(BF)


def attention_specs(steps):
    def column(shift):
        return pl.BlockSpec((BLOCK, PAIR), lambda i: (0, i + shift))

    smem = pl.BlockSpec(memory_space=pltpu.SMEM)
    return [smem, smem, column(0), column(steps), column(2 * steps)] + [
        column(0), column(steps), column(0), column(steps),
        pl.BlockSpec((MPOS // PIECE, 2, PIECE, MPOS), lambda i: (0, i, 0, 0)),
    ]


def window_scratch(count):
    return [pltpu.VMEM((3 * BLOCK, PAIR), F32) for _ in range(count)]


def attend(extents, info, qkv, low, high, table):
    steps = qkv.shape[1] // (3 * PAIR)
    return pl.pallas_call(
        forward_kernel,
        grid=(steps,),
        in_specs=attention_specs(steps),
        out_specs=pl.BlockSpec((BLOCK, PAIR), lambda i: (0, i)),
        out_shape=jax.ShapeDtypeStruct((BLOCK, steps * PAIR), BF),
        scratch_shapes=window_scratch(4) + [pltpu.VMEM((MPOS, PAIR), BF) for _ in range(2)],
        name="attend",
    )(extents, info, qkv, qkv, qkv, low, low, high, high, table)


def attend_back(extents, info, qkv, low, high, table, grads):
    steps = qkv.shape[1] // (3 * PAIR)
    narrow = pl.BlockSpec((BLOCK, PAIR), lambda i: (0, i))
    wide = pl.BlockSpec((3 * BLOCK, PAIR), lambda i: (0, i))
    return pl.pallas_call(
        backward_kernel,
        grid=(steps,),
        in_specs=attention_specs(steps) + [narrow],
        out_specs=[narrow, wide, wide, pl.BlockSpec((2, MPOS, MPOS), lambda i: (i, 0, 0))],
        out_shape=[
            jax.ShapeDtypeStruct((BLOCK, steps * PAIR), BF),
            jax.ShapeDtypeStruct((3 * BLOCK, steps * PAIR), BF),
            jax.ShapeDtypeStruct((3 * BLOCK, steps * PAIR), BF),
            jax.ShapeDtypeStruct((2 * steps, MPOS, MPOS), BF),
        ],
        scratch_shapes=window_scratch(7)
        + [pltpu.VMEM((2, MPOS, MPOS), F32)]
        + [pltpu.VMEM((MPOS, PAIR), BF) for _ in range(2)]
        + [pltpu.VMEM((MPOS, PAIR), F32) for _ in range(2)],
        name="attend_back",
    )(extents, info, qkv, qkv, qkv, low, low, high, high, table, grads)


def swapped(value):
    return lax.ppermute(value, "seq", [(0, 1), (1, 0)])


def crossed(value, bit):
    count = lax.axis_size("fsdp")
    return lax.ppermute(value, "fsdp", [(i, i ^ (1 << bit)) for i in range(count)])


def from_neighbour(value, steps):
    count = lax.axis_size("fsdp")
    leading, last = (max(0, -steps), min(count, count - steps))
    return lax.ppermute(value, "fsdp", [(i, i + steps) for i in range(leading, last)])


def in_order(mine, other, side, axis):
    return jnp.where(
        side == 0,
        jnp.concatenate([mine, other], axis=axis),
        jnp.concatenate([other, mine], axis=axis),
    )


def bits_of(count):
    return count.bit_length() - 1


def gathered(value):
    count = lax.axis_size("fsdp")
    inner = 4
    outer = count // inner
    far = [[a * inner + b for a in range(outer)] for b in range(inner)]
    near = [[a * inner + b for b in range(inner)] for a in range(outer)]
    value = lax.all_gather(value, "fsdp", axis=0, axis_index_groups=far)
    value = lax.all_gather(value, "fsdp", axis=0, axis_index_groups=near)
    return jnp.swapaxes(value, 0, 1).reshape((count,) + value.shape[2:])


def spread(value, own):
    count = lax.axis_size("fsdp")
    total = bits_of(count)
    order = list(range(total - 1, 1, -1)) + [1, 0]
    value = value[None]
    for bit in order:
        value = jnp.concatenate([value, crossed(value, bit)], axis=0)
    away = own ^ jnp.arange(count, dtype=jnp.int32)
    place = sum(((away >> bit) & 1) << rank for rank, bit in enumerate(order))
    return value, place


def summed_part(value, own, axis):
    count = lax.axis_size("fsdp")
    total = bits_of(count)
    shape = value.shape
    value = value.reshape(shape[:axis] + (2,) * total + shape[axis + 1 :])
    left = list(range(total - 1, -1, -1))
    for bit in [0, 1] + list(range(total - 1, 1, -1)):
        at = axis + left.index(bit)
        mine = (own >> bit) & 1
        keep = lax.dynamic_index_in_dim(value, mine, axis=at, keepdims=False)
        send = lax.dynamic_index_in_dim(value, 1 - mine, axis=at, keepdims=False)
        value = keep.astype(F32) + crossed(send.astype(BF), bit).astype(F32)
        left.remove(bit)
    return value


def per_device(
    incoming_state,
    projection_matrix_triple,
    merge_matrix,
    widen_matrix,
    shrink_matrix,
    offset_table,
    norm_scales,
    widen_offset,
    trainable_gate_scores,
    gate_perturbation,
    softening_scale,
    passage_extents,
    result_cotangent,
):
    tok_rows = incoming_state.shape[1]
    tokens = incoming_state.reshape(tok_rows, D)
    seq_count = lax.axis_size("seq")
    shards = lax.axis_size("fsdp")
    devices = seq_count * shards
    head_width = D // seq_count
    group_rows = tok_rows * seq_count
    rows = D // devices
    up_cols = widen_matrix.shape[1]
    blocks = up_cols // D
    side = lax.axis_index("seq")
    own = lax.axis_index("fsdp")

    small = jnp.concatenate([offset_table[2:].reshape(-1), norm_scales.reshape(-1), widen_offset])
    small_row = jnp.pad(small[None], ((0, 7), (0, D - small.shape[0])))
    pack = jnp.concatenate(
        [merge_matrix]
        + [widen_matrix[:, k * D : (k + 1) * D] for k in range(blocks)]
        + [shrink_matrix, small_row],
        axis=0,
    )
    everyone = lax.all_gather(pack, BOTH, axis=0)

    triple = projection_matrix_triple.reshape(rows, 3, seq_count, head_width)
    kept = lax.dynamic_index_in_dim(triple, side, 2, keepdims=False).reshape(rows, 3 * head_width)
    sent = lax.dynamic_index_in_dim(triple, 1 - side, 2, keepdims=False)
    other = swapped(sent.reshape(rows, 3 * head_width))
    block_tokens = in_order(tokens, swapped(tokens), side, 0)
    qv_bias = jnp.concatenate([offset_table[0], offset_table[1]])
    bias_row = jnp.pad(qv_bias[None], ((0, 7), (0, 3 * head_width - 2 * rows)))
    share = jnp.concatenate([in_order(kept, other, side, 0), bias_row], axis=0)
    shares = gathered(share)
    heads_matrix = (
        shares[:, : seq_count * rows]
        .reshape(shards, seq_count, rows, 3 * head_width)
        .swapaxes(0, 1)
        .reshape(D, 3 * head_width)
    )
    q_bias = shares[:, seq_count * rows, :rows].reshape(-1)
    v_bias = shares[:, seq_count * rows, rows : 2 * rows].reshape(-1)
    heads_bias = jnp.concatenate([q_bias, jnp.zeros_like(q_bias), v_bias]).astype(F32)

    relaxed_mask_rows = jax.nn.sigmoid(
        (trainable_gate_scores + gate_perturbation) / softening_scale[:, None, None]
    )
    pieces = MPOS // PIECE
    if relaxed_mask_rows.shape[1] == PIECE:
        table, place = spread(relaxed_mask_rows.astype(BF), own)
    else:
        table = lax.all_gather(relaxed_mask_rows.astype(BF), "fsdp", axis=1, tiled=True)
        table = table.reshape(table.shape[0], pieces, PIECE, MPOS).swapaxes(0, 1)
        place = jnp.arange(pieces, dtype=jnp.int32)
    info = jnp.concatenate([(own * group_rows)[None].astype(jnp.int32), place])

    qkv = (plain_dot(block_tokens, heads_matrix) + heads_bias).astype(BF)
    pair = qkv[:, head_width:]
    low = from_neighbour(pair, 1)
    high = from_neighbour(pair, -1)
    context = attend(passage_extents, info, qkv, low, high, table)

    def rows_of(value, which):
        return lax.dynamic_slice_in_dim(value, which * tok_rows, tok_rows, axis=0)

    context_tok = in_order(
        rows_of(context, side), swapped(rows_of(context, 1 - side)), side, 1
    )

    full_out = everyone[:, :rows].reshape(D, D)
    full_up = jnp.concatenate(
        [everyone[:, (k + 1) * rows : (k + 2) * rows].reshape(D, D) for k in range(blocks)], axis=1
    )
    at = (blocks + 1) * rows
    full_down = everyone[:, at : at + blocks * rows].reshape(up_cols, D)
    smalls = everyone[:, at + blocks * rows, : small.shape[0]].astype(F32)
    vectors = smalls[:, : 6 * rows].reshape(devices, 6, rows).swapaxes(0, 1).reshape(6, D)
    out_bias, down_bias, shift_a, shift_b, gain_a, gain_b = [vectors[k] for k in range(6)]
    up_bias = smalls[:, 6 * rows :].reshape(-1)

    hidden_one = tokens.astype(F32) + (plain_dot(context_tok, full_out) + out_bias)
    normed, norm_one_pull = jax.vjp(layer_norm, hidden_one, gain_a, shift_a)
    normed_low = normed.astype(BF)
    up = plain_dot(normed_low, full_up) + up_bias
    act, gelu_pull = jax.vjp(partial(jax.nn.gelu, approximate=False), up)
    act_low = act.astype(BF)
    hidden_two = normed + (plain_dot(act_low, full_down) + down_bias)
    out, norm_two_pull = jax.vjp(layer_norm, hidden_two, gain_b, shift_b)
    layer_out = out.astype(BF)

    out_cot = result_cotangent.reshape(tok_rows, D).astype(F32)
    grad_two, gain_two, shift_two = norm_two_pull(out_cot)
    down_low = grad_two.astype(BF)
    up_low = gelu_pull(right_dot(down_low, full_down))[0].astype(BF)
    grad_normed = grad_two + right_dot(up_low, full_up)
    grad_one, gain_one, shift_one = norm_one_pull(grad_normed)
    attn_low = grad_one.astype(BF)
    context_grad = right_dot(attn_low, full_out).astype(BF)

    def columns_of(value, which):
        return lax.dynamic_slice_in_dim(value, which * head_width, head_width, axis=1)

    grad_heads = in_order(
        columns_of(context_grad, side), swapped(columns_of(context_grad, 1 - side)), side, 0
    )

    def shares_of(value):
        return value.astype(BF).reshape(devices, -1, D)

    grad_w_down = left_dot(act_low, down_low)
    grad_w_up = left_dot(normed_low, up_low)
    grad_w_out = left_dot(context_tok, attn_low)
    sums = [
        jnp.sum(attn_low.astype(F32), axis=0),
        jnp.sum(down_low.astype(F32), axis=0),
        shift_one,
        shift_two,
        gain_one,
        gain_two,
        jnp.sum(up_low.astype(F32), axis=0),
    ]
    sum_row = jnp.concatenate([value.reshape(devices, -1) for value in sums], axis=1).astype(BF)
    sum_row = jnp.pad(sum_row[:, None], ((0, 0), (0, 7), (0, D - sum_row.shape[1])))
    grads = jnp.concatenate(
        [shares_of(grad_w_out)]
        + [shares_of(grad_w_up[:, k * D : (k + 1) * D]) for k in range(blocks)]
        + [shares_of(grad_w_down), sum_row],
        axis=1,
    )
    early = lax.psum_scatter(grads, BOTH, scatter_dimension=0)

    query_grad, key_grad, value_grad, table_grad = attend_back(
        passage_extents, info, qkv, low, high, table, grad_heads
    )
    window_grad = jnp.concatenate([key_grad, value_grad], axis=1)
    from_right = from_neighbour(window_grad[:group_rows], -1)
    from_left = from_neighbour(window_grad[2 * group_rows :], 1)
    pair_grad = (
        window_grad[group_rows : 2 * group_rows].astype(F32)
        + from_right.astype(F32)
        + from_left.astype(F32)
    ).astype(BF)
    heads_grad = jnp.concatenate([query_grad, pair_grad], axis=1)

    heads_matrix_grad = (
        left_dot(block_tokens, heads_grad)
        .astype(BF)
        .reshape(seq_count, shards, rows, 3 * head_width)
        .swapaxes(0, 1)
        .reshape(shards, seq_count * rows, 3 * head_width)
    )
    column_sums = jnp.sum(heads_grad.astype(F32), axis=0).astype(BF)
    qv_sums = jnp.concatenate(
        [
            column_sums[:head_width].reshape(shards, rows),
            column_sums[2 * head_width :].reshape(shards, rows),
        ],
        axis=1,
    )
    qv_row = jnp.pad(qv_sums[:, None], ((0, 0), (0, 7), (0, 3 * head_width - 2 * rows)))
    late = summed_part(jnp.concatenate([heads_matrix_grad, qv_row], axis=1), own, 0)
    late_rows = late[: seq_count * rows].reshape(seq_count, rows, 3 * head_width)
    late_mine = lax.dynamic_index_in_dim(late_rows, side, 0, keepdims=False)
    late_other = swapped(lax.dynamic_index_in_dim(late_rows, 1 - side, 0, keepdims=False).astype(BF))
    grad_w_qkv = in_order(
        late_mine.reshape(rows, 3, 1, head_width),
        late_other.astype(F32).reshape(rows, 3, 1, head_width),
        side,
        2,
    ).reshape(rows, 3 * D)
    qv_total = late[seq_count * rows, : 2 * rows].reshape(2, rows)

    partial_input = right_dot(heads_grad, heads_matrix)
    input_grad = (
        grad_one
        + rows_of(partial_input, side)
        + swapped(rows_of(partial_input, 1 - side).astype(BF)).astype(F32)
    )

    table_rows_each = MPOS // shards
    table_total = summed_part(
        table_grad.reshape(table_grad.shape[0], shards, table_rows_each, MPOS), own, 1
    )
    mask_logit_gradient = (
        table_total
        * relaxed_mask_rows
        * (1.0 - relaxed_mask_rows)
        / softening_scale[:, None, None]
    )
    early = early.astype(F32)
    totals = early[at + blocks * rows, : 6 * rows + blocks * rows]
    named = totals[: 6 * rows].reshape(6, rows)
    return (
        layer_out.reshape(1, tok_rows, D),
        input_grad.reshape(1, tok_rows, D),
        grad_w_qkv,
        early[:rows],
        jnp.concatenate([early[(k + 1) * rows : (k + 2) * rows] for k in range(blocks)], axis=1),
        early[at : at + blocks * rows],
        jnp.concatenate([qv_total, named[:4]], axis=0),
        named[4:6],
        totals[6 * rows :],
        mask_logit_gradient,
    )


def solution(mesh):
    return jax.shard_map(
        per_device,
        mesh=mesh,
        in_specs=(
            P("fsdp", "seq", None),
            P(("seq", "fsdp"), None),
            P(("seq", "fsdp"), None),
            P(("seq", "fsdp"), None),
            P(("seq", "fsdp"), None),
            P(None, ("seq", "fsdp")),
            P(None, ("seq", "fsdp")),
            P(("seq", "fsdp")),
            P("seq", "fsdp", None),
            P("seq", "fsdp", None),
            P("seq"),
            P(),
            P("fsdp", "seq", None),
        ),
        out_specs=(
            P("fsdp", "seq", None),
            P("fsdp", "seq", None),
            P(("seq", "fsdp"), None),
            P(("seq", "fsdp"), None),
            P(("seq", "fsdp"), None),
            P(("seq", "fsdp"), None),
            P(None, ("seq", "fsdp")),
            P(None, ("seq", "fsdp")),
            P(("seq", "fsdp")),
            P("seq", "fsdp", None),
        ),
        check_vma=False,
    )
```
